1024 devices in a mesh: row: 32 (over z), col: 32 (over y, x, core).
Axes of the slice: x: 4, y: 4, z: 32, core: 2. Of those that a mesh axis runs over, the one named last changes fastest.
Arguments:
- amplitudes: bfloat16 [32, 256, 64, 2048], P(None, 'col', 'row'), may hold values from -6 to 6
- integrals: bfloat16 [8, 64, 32, 64], P(None, None, 'col'), may hold values from -0.125 to 0.125
- others: bfloat16 [8, 256, 64, 2048], P(None, 'col', 'row'), may hold values from -6 to 6
- occupied_left: float32 [8], replicated, may hold values from -1.5 to -0.3
- occupied_right: float32 [256], P('col'), may hold values from -1.5 to -0.3
- virtual_left: float32 [64], P('row'), may hold values from 0.2 to 3
- virtual_right: float32 [2048], replicated, may hold values from 0.2 to 3
- tile_mask: int32 [4, 32], replicated, may hold values 0 or 1
Outputs:
- update: bfloat16 [8, 256, 64, 2048], P(None, 'col', 'row')
The draws below stay inside these ranges and needn't reach their ends.
All inputs are finite; a program needn't handle non-finite values.
Results may differ from the reference program's by a relative error of at most 0.0039.
Values may be sent and summed in bfloat16 or wider, within the bound.
No kernel may reach another device: no remote copies, remote signals or barrier semaphores. Data moves between devices by JAX's collectives and lax.ppermute only.
A program may use at most 64 MiB of HBM per device.

```python
import jax
import jax.numpy as jnp
from jax import lax

TILE = 64
IO = 8
JT = 4
KO = 32
JO = 256
BV = 2048
N_ROW = 32


def place_ends(drawn, rng, smallest, high):
    extent = drawn.shape
    place = [jax.random.randint(jax.random.fold_in(rng, axis), (), 0, extent[axis]) for axis in range(len(extent))]
    drawn = drawn.at[tuple(place)].set(smallest)
    longest = extent.index(max(extent))
    place[longest] = (place[longest] + 1) % extent[longest]
    return drawn.at[tuple(place)].set(high)


def shard_levels(own_key, dims, split, least, largest):
    def one(position, shards_of):
        steps = jax.random.uniform(jax.random.fold_in(jax.random.fold_in(own_key, 6), position), (shards_of,), jnp.float32, least / len(split), largest / len(split))
        return jnp.repeat(jnp.exp(steps), dims[position] // shards_of).reshape((-1,) + (1,) * (len(dims) - position - 1))

    factor_of = one(*split[0])
    for cut in split[1:]:
        factor_of = factor_of * one(*cut)
    return factor_of


def bell_draw(rng, dims, scale, reach, shards=(), kind=jnp.bfloat16):
    gain = shard_levels(rng, dims, shards, -0.22, 0.18) if shards else 1.0
    values = jax.random.normal(rng, dims, jnp.float32) * scale * gain
    return jnp.minimum(jnp.maximum(values, -reach), reach).astype(kind)


def setup_inputs(seed: int = 0) -> dict:
    streams_of = jax.random.split(jax.random.key(seed), 9)
    amplitudes = bell_draw(streams_of[0], (KO, JO, TILE, BV), 1.0, 6.0, ((1, 32), (2, 32)))
    integrals = bell_draw(streams_of[1], (IO, TILE, KO, TILE), (KO * TILE) ** -0.5, 0.125, ((2, 32),))
    others = bell_draw(streams_of[2], (IO, JO, TILE, BV), 1.0, 6.0, ((1, 32), (2, 32)))
    occupied_left = jnp.clip(jax.random.uniform(streams_of[3], (IO,), jnp.float32, -1.5, -0.3), -1.5, -0.3)
    occupied_right = jnp.clip(-1.5 + 1.2 * jax.random.uniform(streams_of[4], (JO,), jnp.float32) ** shard_levels(streams_of[4], (JO,), ((0, 32),), -0.2, 0.2), -1.5, -0.3)
    virtual_left = jnp.clip(0.2 + 2.8 * jax.random.uniform(streams_of[5], (TILE,), jnp.float32) ** shard_levels(streams_of[5], (TILE,), ((0, 32),), -0.2, 0.2), 0.2, 3.0)
    virtual_right = jnp.clip(jax.random.uniform(streams_of[6], (BV,), jnp.float32, 0.2, 3.0), 0.2, 3.0)
    tile_mask = place_ends((jax.random.randint(streams_of[7], (JT, N_ROW), 0, 2) < 1).astype(jnp.int32), jax.random.fold_in(streams_of[7], 1), 0, 1)
    return {"amplitudes": amplitudes, "integrals": integrals, "others": others, "occupied_left": occupied_left, "occupied_right": occupied_right, "virtual_left": virtual_left, "virtual_right": virtual_right, "tile_mask": tile_mask}


def reference(amplitudes, integrals, others, occupied_left, occupied_right, virtual_left, virtual_right, tile_mask):
    tile_count = virtual_right.shape[0] // TILE
    left_f32 = integrals.astype(jnp.float32)

    def one_tile(tile_index):
        offset = (tile_index * TILE).astype(jnp.int32)
        amp_block = lax.dynamic_slice_in_dim(amplitudes, offset, TILE, 3).astype(jnp.float32)
        cycle_term = jnp.einsum("iakc,kjcb->ijab", left_f32, amp_block).astype(jnp.bfloat16)
        cycle_term = lax.optimization_barrier(cycle_term)
        carried = lax.dynamic_slice_in_dim(others, offset, TILE, 3).astype(jnp.float32)
        energy_b = lax.dynamic_slice_in_dim(virtual_right, offset, TILE, 0)
        denominator = (occupied_left[:, None, None, None] + occupied_right[None, :, None, None]
                       - virtual_left[None, None, :, None] - energy_b[None, None, None, :])
        mask_line = lax.dynamic_index_in_dim(tile_mask, tile_index, 1, keepdims=False)
        keep = jnp.repeat(mask_line.astype(jnp.float32), TILE)
        result = keep[None, :, None, None] * (carried + cycle_term.astype(jnp.float32)) / denominator
        return result.astype(jnp.bfloat16)

    stacked = lax.map(one_tile, jnp.arange(tile_count, dtype=jnp.int32))
    moved = jnp.moveaxis(stacked, 0, 3)
    return moved.reshape(moved.shape[0], moved.shape[1], moved.shape[2], tile_count * TILE)
```

```python
import functools

import jax
import jax.numpy as jnp
from jax import lax
from jax.experimental import pallas as pl
from jax.experimental.pallas import tpu as pltpu
from jax.sharding import PartitionSpec as P

TILE = 64
LANES = 128
ROWS = 32
NI = 8
NJ = 8
NK = 32
BV = 2048
NB = BV // TILE
KEEP_CAPS = (20, 24, 32)


def swap(v):
    return jnp.concatenate([v[..., TILE:], v[..., :TILE]], axis=-1)


def low_half(shape):
    return lax.broadcasted_iota(jnp.int32, shape, len(shape) - 1) < TILE


def list_kept(mask_ref, jt, idx_ref, pos_ref):
    if idx_ref is not None:
        for t in range(NB):
            idx_ref[t] = 0
    count = jnp.int32(0)
    for b in range(NB):
        if idx_ref is not None:
            idx_ref[count] = b
        if pos_ref is not None:
            pos_ref[b] = count
        count = count + jnp.minimum(mask_ref[jt, b], 1)


def pack_kernel(cap, mask_ref, jt_ref, x_ref, o_ref, xs_ref, idx_ref):
    full = cap // 8

    @pl.when(pl.program_id(0) == 0)
    def _():
        list_kept(mask_ref, jt_ref[0], idx_ref, None)

    xs_ref[...] = x_ref[:, 0].reshape(2 * NK, BV)

    def lanes_of(tile):
        return xs_ref[:, pl.ds(pl.multiple_of((tile // 2) * LANES, LANES), LANES)]

    def low(v, tile):
        return jnp.where(tile % 2 == 0, v, swap(v))

    def high(v, tile):
        return jnp.where(tile % 2 == 1, v, swap(v))

    for u in range(full):
        for q in range(4):
            t0 = idx_ref[8 * u + 2 * q]
            t1 = idx_ref[8 * u + 2 * q + 1]
            a = low(lanes_of(t0), t0)
            b = high(lanes_of(t1), t1)
            o_ref[q, 64 * u : 64 * u + 64, :] = jnp.concatenate([a[:, :TILE], b[:, TILE:]], axis=1)
    if cap % 8:
        for q in range(4):
            t0 = idx_ref[8 * full + q]
            v = lanes_of(t0)
            a = low(v[:32], t0)
            b = high(v[32:], t0)
            o_ref[q, 64 * full :, :] = jnp.concatenate([a[:, :TILE], b[:, TILE:]], axis=1)


def contract_kernel(cap, r_ref, w_ref, o_ref, x_ref):
    full = cap // 8
    for u in range(full):
        x_ref[:, LANES * u : LANES * (u + 1)] = r_ref[:, 64 * u : 64 * u + 64, :].reshape(ROWS * 64, LANES)
    if cap % 8:
        y = r_ref[:, 64 * full :, :]
        m = low_half(y.shape)
        z = jnp.zeros_like(y)
        both = jnp.concatenate([jnp.where(m, y, z), jnp.where(m, z, y)], axis=1)
        x_ref[:, LANES * full :] = both.reshape(ROWS * 64, LANES)
    p = jnp.dot(w_ref[...], x_ref[...], preferred_element_type=jnp.float32)
    for u in range(full):
        part = p[:, LANES * u : LANES * (u + 1)].reshape(ROWS, 16, LANES)
        o_ref[:, 16 * u : 16 * u + 16, :] = part.astype(jnp.bfloat16)
    if cap % 8:
        part = p[:, LANES * full :]
        part = (part + swap(part)).reshape(ROWS, 2, 8, LANES)
        folded = jnp.where(low_half((ROWS, 8, LANES)), part[:, 0], part[:, 1])
        o_ref[:, 16 * full :, :] = folded.astype(jnp.bfloat16)


def update_kernel(cap, mask_ref, jt_ref, c_ref, oth_ref, row_ref, vr_ref, o_ref, comp_ref, oths_ref, res_ref, pos_ref):
    full = cap // 8
    jt = jt_ref[0]

    @pl.when(pl.program_id(0) == 0)
    def _():
        list_kept(mask_ref, jt, None, pos_ref)

    oths_ref[...] = oth_ref[:, 0].reshape(16, BV).astype(jnp.float32)
    for u in range(full):
        for q in range(4):
            comp_ref[4 * u + q] = c_ref[q, 16 * u : 16 * u + 16, :].astype(jnp.float32)
    if cap % 8:
        m8 = low_half((8, LANES))
        for h in range(2):
            f0 = c_ref[2 * h, 16 * full :, :].astype(jnp.float32)
            f1 = c_ref[2 * h + 1, 16 * full :, :].astype(jnp.float32)
            comp_ref[4 * full + h, 0:8, :] = jnp.where(m8, f0, swap(f1))
            comp_ref[4 * full + h, 8:16, :] = jnp.where(m8, swap(f0), f1)
    m16 = low_half((16, LANES))
    row = row_ref[0]
    for lt in range(BV // LANES):
        sl = slice(LANES * lt, LANES * (lt + 1))
        p0 = jnp.minimum(pos_ref[2 * lt], cap - 1)
        p1 = jnp.minimum(pos_ref[2 * lt + 1], cap - 1)
        c0 = comp_ref[p0 // 2]
        c1 = comp_ref[p1 // 2]
        a = jnp.where(p0 % 2 == 0, c0, swap(c0))
        b = jnp.where(p1 % 2 == 1, c1, swap(c1))
        k0 = mask_ref[jt, 2 * lt].astype(jnp.float32)
        k1 = mask_ref[jt, 2 * lt + 1].astype(jnp.float32)
        keep = jnp.where(m16, k0, k1)
        cycle = jnp.where(m16, a, b)
        denominator = row - vr_ref[:, sl]
        res_ref[:, sl] = keep * (oths_ref[:, sl] + cycle) / denominator
    o_ref[...] = res_ref[...].reshape(NI, 2, BV).astype(jnp.bfloat16)[:, None]


def one_cap(cap, amplitudes, integrals, others, row_term, virtual_right, tile_mask, jt):
    full, half = divmod(cap, 8)
    half = int(half > 0)
    rows_in = 64 * full + 32 * half
    rows_out = 16 * full + 8 * half
    bf16 = jnp.bfloat16
    whole = pl.BlockSpec(memory_space=pltpu.VMEM)
    packed = pl.pallas_call(
        functools.partial(pack_kernel, cap),
        out_shape=jax.ShapeDtypeStruct((ROWS, rows_in, LANES), bf16),
        grid_spec=pltpu.PrefetchScalarGridSpec(
            num_scalar_prefetch=2,
            grid=(NJ,),
            in_specs=[pl.BlockSpec((NK, 1, 2, BV), lambda j, m, t: (0, j, 0, 0))],
            out_specs=pl.BlockSpec((4, rows_in, LANES), lambda j, m, t: (j, 0, 0)),
            scratch_shapes=[pltpu.VMEM((2 * NK, BV), bf16), pltpu.SMEM((NB,), jnp.int32)],
        ),
        name="pack",
    )(tile_mask, jt, amplitudes)
    received = lax.all_to_all(packed, "row", split_axis=0, concat_axis=0, tiled=True)

    own = integrals[:, :, 0, :].reshape(NI, ROWS, 2, TILE).transpose(3, 1, 0, 2).reshape(TILE, NI * TILE)
    gathered = lax.all_gather(own, "col", axis=0, tiled=False)
    by_row = gathered.reshape(NK, ROWS, 2, NI * TILE).transpose(1, 0, 2, 3).reshape(NK * TILE, NI * TILE)
    weights = by_row.T

    cycle = pl.pallas_call(
        functools.partial(contract_kernel, cap),
        out_shape=jax.ShapeDtypeStruct((ROWS, rows_out, LANES), bf16),
        in_specs=[whole, whole],
        out_specs=whole,
        scratch_shapes=[pltpu.VMEM((NK * TILE, LANES * (full + half)), bf16)],
        compiler_params=pltpu.CompilerParams(vmem_limit_bytes=40 << 20),
        name="contract",
    )(received, weights)
    returned = lax.all_to_all(cycle, "row", split_axis=0, concat_axis=0, tiled=True)

    return pl.pallas_call(
        functools.partial(update_kernel, cap),
        out_shape=jax.ShapeDtypeStruct(others.shape, bf16),
        grid_spec=pltpu.PrefetchScalarGridSpec(
            num_scalar_prefetch=2,
            grid=(NJ,),
            in_specs=[
                pl.BlockSpec((4, rows_out, LANES), lambda j, m, t: (j, 0, 0)),
                pl.BlockSpec((NI, 1, 2, BV), lambda j, m, t: (0, j, 0, 0)),
                pl.BlockSpec((1, 16, LANES), lambda j, m, t: (j, 0, 0)),
                pl.BlockSpec((1, BV), lambda j, m, t: (0, 0)),
            ],
            out_specs=pl.BlockSpec((NI, 1, 2, BV), lambda j, m, t: (0, j, 0, 0)),
            scratch_shapes=[
                pltpu.VMEM((cap // 2, 16, LANES), jnp.float32),
                pltpu.VMEM((16, BV), jnp.float32),
                pltpu.VMEM((16, BV), jnp.float32),
                pltpu.SMEM((NB,), jnp.int32),
            ],
        ),
        name="update",
    )(tile_mask, jt, returned, others, row_term, virtual_right[None])


def shards(
    amplitudes,
    integrals,
    others,
    occupied_left,
    occupied_right,
    virtual_left,
    virtual_right,
    tile_mask,
):
    jt = (lax.axis_index("col") * NJ // TILE).astype(jnp.int32).reshape(1)
    row_term = (
        occupied_left[None, :, None] + occupied_right[:, None, None] - virtual_left[None, None, :]
    ).reshape(NJ, NI * 2)
    row_term = jnp.broadcast_to(row_term[:, :, None], (NJ, NI * 2, LANES))
    most = jnp.max(jnp.sum(jnp.minimum(tile_mask, 1), axis=1))
    branch = jnp.sum((most > jnp.array(KEEP_CAPS[:-1], jnp.int32)).astype(jnp.int32))
    return lax.switch(
        branch,
        [functools.partial(one_cap, cap) for cap in KEEP_CAPS],
        amplitudes,
        integrals,
        others,
        row_term,
        virtual_right,
        tile_mask,
        jt,
    )


def solution(mesh):
    in_specs = (
        P(None, "col", "row", None),
        P(None, None, "col", None),
        P(None, "col", "row", None),
        P(),
        P("col"),
        P("row"),
        P(),
        P(),
    )
    out_specs = P(None, "col", "row", None)
    return jax.shard_map(shards, mesh=mesh, in_specs=in_specs, out_specs=out_specs, check_vma=False)
```

```python
import functools

import jax
import jax.numpy as jnp
from jax import lax
from jax.experimental import pallas as pl
from jax.experimental.pallas import tpu as pltpu
from jax.sharding import PartitionSpec as P

TILE = 64
LANES = 128
ROWS = 32
NI = 8
NJ = 8
NK = 32
BV = 2048
NB = BV // TILE
KEEP_CAPS = (18, 20, 24)


def turn(v, by):
    by %= LANES
    return v if by == 0 else jnp.concatenate([v[..., LANES - by :], v[..., : LANES - by]], axis=-1)


def lane_group(shape, width):
    return lax.broadcasted_iota(jnp.int32, shape, len(shape) - 1) // width


def pieces(cap):
    found = []
    tile, row_in, row_out = 0, 0, 0
    for step, fold in [(8, 1)] * (cap // 8) + [(4, 2)] * (cap % 8 // 4) + [(2, 4)] * (cap % 4 // 2):
        found.append((tile, fold, row_in, row_out))
        tile, row_in, row_out = tile + step, row_in + 64 // fold, row_out + 16 // fold
    return found, row_in, row_out


def list_kept(mask_ref, jt, idx_ref, pos_ref):
    if idx_ref is not None:
        for t in range(2 * NB):
            idx_ref[t] = 0
    count = jnp.int32(0)
    for b in range(NB):
        if idx_ref is not None:
            idx_ref[count] = b
        if pos_ref is not None:
            pos_ref[b] = count
        count = count + jnp.minimum(mask_ref[jt, b], 1)


def pack_kernel(cap, mask_ref, jt_ref, x_ref, o_ref, xs_ref, idx_ref):
    @pl.when(pl.program_id(0) == 0)
    def _():
        list_kept(mask_ref, jt_ref[0], idx_ref, None)

    xs_ref[...] = x_ref[:, 0].reshape(2 * NK, BV)

    def lanes_of(tile):
        return xs_ref[:, pl.ds(pl.multiple_of((tile // 2) * LANES, LANES), LANES)]

    def low(v, tile):
        return jnp.where(tile % 2 == 0, v, turn(v, TILE))

    def high(v, tile):
        return jnp.where(tile % 2 == 1, v, turn(v, TILE))

    first = jt_ref[1]
    for tile, fold, row, _ in pieces(cap)[0]:
        for q in range(4):
            if fold == 1:
                t0 = idx_ref[first + tile + 2 * q]
                t1 = idx_ref[first + tile + 2 * q + 1]
                parts = [low(lanes_of(t0), t0)[:, :TILE], high(lanes_of(t1), t1)[:, TILE:]]
            elif fold == 2:
                t0 = idx_ref[first + tile + q]
                v = lanes_of(t0)
                parts = [low(v[:32], t0)[:, :TILE], high(v[32:], t0)[:, TILE:]]
            else:
                t0 = idx_ref[first + tile + q // 2]
                v = low(lanes_of(t0), t0)
                parts = [turn(v[16 * g : 16 * g + 16], 32 * (g - q % 2))[:, 32 * g : 32 * g + 32] for g in range(4)]
            o_ref[q, row : row + 64 // fold, :] = jnp.concatenate(parts, axis=1)


def contract_kernel(cap, r_ref, w_ref, o_ref, x_ref):
    found = pieces(cap)[0]
    for n, (_, fold, row, _) in enumerate(found):
        y = r_ref[:, row : row + 64 // fold, :]
        if fold > 1:
            group = lane_group(y.shape, LANES // fold)
            y = jnp.concatenate([jnp.where(group == g, y, jnp.zeros_like(y)) for g in range(fold)], axis=1)
        x_ref[:, LANES * n : LANES * (n + 1)] = y.reshape(ROWS * 64, LANES)
    p = jnp.dot(w_ref[...], x_ref[...], preferred_element_type=jnp.float32)
    for n, (_, fold, _, row) in enumerate(found):
        part = p[:, LANES * n : LANES * (n + 1)]
        if fold > 1:
            part = part + turn(part, 64)
        if fold > 2:
            part = part + turn(part, 32)
        height = 16 // fold
        part = part.reshape(ROWS, 16, LANES)
        out = part[:, :height]
        group = lane_group(out.shape, LANES // fold)
        for g in range(1, fold):
            out = jnp.where(group == g, part[:, height * g : height * (g + 1)], out)
        o_ref[:, row : row + height, :] = out.astype(jnp.bfloat16)


def prepare_kernel(mask_ref, jt_ref, oth_ref, row_ref, vr_ref, oths_ref, factor_ref):
    jt = jt_ref[0]
    low = lane_group((16, LANES), TILE) == 0

    def one_j(j, carry):
        oths_ref[j] = oth_ref[:, j].reshape(16, BV)
        row = row_ref[j]
        for lt in range(BV // LANES):
            sl = slice(LANES * lt, LANES * (lt + 1))
            k0 = mask_ref[jt, 2 * lt].astype(jnp.float32)
            k1 = mask_ref[jt, 2 * lt + 1].astype(jnp.float32)
            factor_ref[j, :, sl] = jnp.where(low, k0, k1) / (row - vr_ref[:, sl])
        return carry

    lax.fori_loop(0, NJ, one_j, 0)


def update_kernel(cap, repeated, mask_ref, jt_ref, c_ref, oths_ref, factor_ref, *refs):
    if repeated:
        before_ref, *refs = refs
    o_ref, comp_ref, res_ref, pos_ref = refs
    first = jt_ref[1]
    found = pieces(cap)[0]
    list_kept(mask_ref, jt_ref[0], None, pos_ref)
    low = lane_group((16, LANES), TILE) == 0

    def one_j(j, carry):
        for tile, fold, _, row in found:
            blocks = [c_ref[4 * j + q, row : row + 16 // fold, :].astype(jnp.float32) for q in range(4)]
            if fold == 1:
                for q in range(4):
                    comp_ref[tile // 2 + q] = blocks[q]
            elif fold == 2:
                m = lane_group((8, LANES), TILE) == 0
                for h in range(2):
                    f0, f1 = blocks[2 * h], blocks[2 * h + 1]
                    comp_ref[tile // 2 + h, 0:8, :] = jnp.where(m, f0, turn(f1, TILE))
                    comp_ref[tile // 2 + h, 8:16, :] = jnp.where(m, turn(f0, TILE), f1)
            else:
                group = lane_group((4, LANES), 32)
                for g in range(4):
                    out = turn(blocks[0], -32 * g)
                    for q in range(1, 4):
                        out = jnp.where(group == q, turn(blocks[q], 32 * (q - g)), out)
                    comp_ref[tile // 2, 4 * g : 4 * g + 4, :] = out
        for lt in range(BV // LANES):
            sl = slice(LANES * lt, LANES * (lt + 1))
            p0 = jnp.clip(pos_ref[2 * lt] - first, 0, cap - 1)
            p1 = jnp.clip(pos_ref[2 * lt + 1] - first, 0, cap - 1)
            a = pltpu.roll(comp_ref[p0 // 2], TILE * (p0 % 2), 1)
            b = pltpu.roll(comp_ref[p1 // 2], TILE * (1 - p1 % 2), 1)
            cycle = jnp.where(low, a, b)
            res_ref[:, sl] = factor_ref[j, :, sl] * (oths_ref[j, :, sl].astype(jnp.float32) + cycle)
        if repeated:
            done = before_ref[:, j].reshape(16, BV).astype(jnp.float32)
            for lt in range(BV // LANES):
                sl = slice(LANES * lt, LANES * (lt + 1))
                d0 = (pos_ref[2 * lt] < first).astype(jnp.int32)
                d1 = (pos_ref[2 * lt + 1] < first).astype(jnp.int32)
                res_ref[:, sl] = jnp.where(jnp.where(low, d0, d1) > 0, done[:, sl], res_ref[:, sl])
        o_ref[:, j] = res_ref[...].reshape(NI, 2, BV).astype(jnp.bfloat16)
        return carry

    lax.fori_loop(0, NJ, one_j, 0)


def one_pass(cap, before, amplitudes, integrals, others, row_term, virtual_right, tile_mask, jt):
    found, rows_in, rows_out = pieces(cap)
    bf16 = jnp.bfloat16
    whole = pl.BlockSpec(memory_space=pltpu.VMEM)
    scalars = pl.BlockSpec(memory_space=pltpu.SMEM)
    packed = pl.pallas_call(
        functools.partial(pack_kernel, cap),
        out_shape=jax.ShapeDtypeStruct((ROWS, rows_in, LANES), bf16),
        grid_spec=pltpu.PrefetchScalarGridSpec(
            num_scalar_prefetch=2,
            grid=(NJ,),
            in_specs=[pl.BlockSpec((NK, 1, 2, BV), lambda j, m, t: (0, j, 0, 0))],
            out_specs=pl.BlockSpec((4, rows_in, LANES), lambda j, m, t: (j, 0, 0)),
            scratch_shapes=[pltpu.VMEM((2 * NK, BV), bf16), pltpu.SMEM((2 * NB,), jnp.int32)],
        ),
        name="pack",
    )(tile_mask, jt, amplitudes)
    received = lax.all_to_all(packed, "row", split_axis=0, concat_axis=0, tiled=True)

    own = integrals[:, :, 0, :].reshape(NI, ROWS, 2, TILE).transpose(3, 1, 0, 2).reshape(TILE, NI * TILE)
    gathered = lax.all_gather(own, "col", axis=0, tiled=False)
    by_row = gathered.reshape(NK, ROWS, 2, NI * TILE).transpose(1, 0, 2, 3).reshape(NK * TILE, NI * TILE)
    weights = by_row.T

    cycle = pl.pallas_call(
        functools.partial(contract_kernel, cap),
        out_shape=jax.ShapeDtypeStruct((ROWS, rows_out, LANES), bf16),
        in_specs=[whole, whole],
        out_specs=whole,
        scratch_shapes=[
            pltpu.VMEM((NK * TILE, LANES * len(found)), bf16),
        ],
        compiler_params=pltpu.CompilerParams(vmem_limit_bytes=40 << 20),
        name="contract",
    )(received, weights)
    returned = lax.all_to_all(cycle, "row", split_axis=0, concat_axis=0, tiled=True)

    residual, factor = pl.pallas_call(
        prepare_kernel,
        out_shape=[
            jax.ShapeDtypeStruct((NJ, 2 * NI, BV), bf16),
            jax.ShapeDtypeStruct((NJ, 2 * NI, BV), jnp.float32),
        ],
        in_specs=[scalars, scalars, whole, whole, whole],
        out_specs=[whole, whole],
        compiler_params=pltpu.CompilerParams(vmem_limit_bytes=40 << 20),
        name="prepare",
    )(tile_mask, jt, others, row_term, virtual_right[None])

    return pl.pallas_call(
        functools.partial(update_kernel, cap, bool(before)),
        out_shape=jax.ShapeDtypeStruct(others.shape, bf16),
        in_specs=[scalars, scalars, whole, whole, whole] + [whole] * len(before),
        out_specs=whole,
        scratch_shapes=[
            pltpu.VMEM((cap // 2, 16, LANES), jnp.float32),
            pltpu.VMEM((16, BV), jnp.float32),
            pltpu.SMEM((NB,), jnp.int32),
        ],
        compiler_params=pltpu.CompilerParams(vmem_limit_bytes=40 << 20),
        name="update",
    )(tile_mask, jt, returned, residual, factor, *before)


def once(cap, most, jt, *arrays):
    return one_pass(cap, [], *arrays, jnp.stack([jt, jnp.int32(0)]))


def repeatedly(cap, most, jt, *arrays):
    def step(n, before):
        return one_pass(cap, [before], *arrays, jnp.stack([jt, n * cap]))

    passes = jnp.maximum((most + cap - 1) // cap, 1)
    return lax.fori_loop(0, passes, step, jnp.zeros_like(arrays[2]))


def shards(
    amplitudes,
    integrals,
    others,
    occupied_left,
    occupied_right,
    virtual_left,
    virtual_right,
    tile_mask,
):
    jt = (lax.axis_index("col") // (TILE // NJ)).astype(jnp.int32)
    row_term = (
        occupied_left[None, :, None] + occupied_right[:, None, None] - virtual_left[None, None, :]
    ).reshape(NJ, NI * 2)
    row_term = jnp.broadcast_to(row_term[:, :, None], (NJ, NI * 2, LANES))
    most = jnp.max(jnp.sum(tile_mask, axis=1))
    branch = sum((most > cap).astype(jnp.int32) for cap in KEEP_CAPS[:-1])
    steps = [functools.partial(once, cap) for cap in KEEP_CAPS[:-1]] + [functools.partial(repeatedly, KEEP_CAPS[-1])]
    return lax.switch(
        branch, steps, most, jt, amplitudes, integrals, others, row_term, virtual_right, tile_mask
    )


def solution(mesh):
    in_specs = (
        P(None, "col", "row", None),
        P(None, None, "col", None),
        P(None, "col", "row", None),
        P(),
        P("col"),
        P("row"),
        P(),
        P(),
    )
    out_specs = P(None, "col", "row", None)
    return jax.shard_map(shards, mesh=mesh, in_specs=in_specs, out_specs=out_specs, check_vma=False)
```

```python
import functools

import jax
import jax.numpy as jnp
from jax import lax
from jax.experimental import pallas as pl
from jax.experimental.pallas import tpu as pltpu
from jax.sharding import PartitionSpec as P

TILE = 64
LANES = 128
ROWS = 32
NI = 8
NJ = 8
NK = 32
PACK_J = 4
BV = 2048
NB = BV // TILE
KEEP_CAPS = (18, 20, 24)


def turn(v, by):
    by %= LANES
    return v if by == 0 else jnp.concatenate([v[..., LANES - by :], v[..., : LANES - by]], axis=-1)


def lane_group(shape, width):
    return lax.broadcasted_iota(jnp.int32, shape, len(shape) - 1) // width


def pieces(cap):
    found = []
    tile, row_in, row_out = 0, 0, 0
    for step, fold in [(8, 1)] * (cap // 8) + [(4, 2)] * (cap % 8 // 4) + [(2, 4)] * (cap % 4 // 2):
        found.append((tile, fold, row_in, row_out))
        tile, row_in, row_out = tile + step, row_in + 64 // fold, row_out + 16 // fold
    return found, row_in, row_out


def list_kept(mask_ref, jt, idx_ref, pos_ref):
    if idx_ref is not None:
        for t in range(2 * NB):
            idx_ref[t] = 0
    count = jnp.int32(0)
    for b in range(NB):
        if idx_ref is not None:
            idx_ref[count] = b
        if pos_ref is not None:
            pos_ref[b] = count
        count = count + jnp.minimum(mask_ref[jt, b], 1)


def choose_kernel(mask_ref, o_ref):
    most = jnp.int32(0)
    for row in range(mask_ref.shape[0]):
        most = jnp.maximum(most, sum(mask_ref[row, b] for b in range(NB)))
    o_ref[0] = sum((most > cap).astype(jnp.int32) for cap in KEEP_CAPS[:-1])
    o_ref[1] = most


def pack_kernel(cap, mask_ref, jt_ref, x_ref, o_ref, xs_ref, idx_ref):
    @pl.when(pl.program_id(0) == 0)
    def _():
        list_kept(mask_ref, jt_ref[0], idx_ref, None)

    def lanes_of(tile):
        return xs_ref[:, pl.ds(pl.multiple_of((tile // 2) * LANES, LANES), LANES)]

    def low(v, tile):
        return jnp.where(tile % 2 == 0, v, turn(v, TILE))

    def high(v, tile):
        return jnp.where(tile % 2 == 1, v, turn(v, TILE))

    first = jt_ref[1]

    def one_j(j, carry):
        xs_ref[...] = x_ref[:, j].reshape(2 * NK, BV)
        for tile, fold, row, _ in pieces(cap)[0]:
            for q in range(4):
                if fold == 1:
                    t0 = idx_ref[first + tile + 2 * q]
                    t1 = idx_ref[first + tile + 2 * q + 1]
                    parts = [low(lanes_of(t0), t0)[:, :TILE], high(lanes_of(t1), t1)[:, TILE:]]
                elif fold == 2:
                    t0 = idx_ref[first + tile + q]
                    v = lanes_of(t0)
                    parts = [low(v[:32], t0)[:, :TILE], high(v[32:], t0)[:, TILE:]]
                else:
                    t0 = idx_ref[first + tile + q // 2]
                    v = low(lanes_of(t0), t0)
                    parts = [turn(v[16 * g : 16 * g + 16], 32 * (g - q % 2))[:, 32 * g : 32 * g + 32] for g in range(4)]
                o_ref[4 * j + q, row : row + 64 // fold, :] = jnp.concatenate(parts, axis=1)
        return carry

    lax.fori_loop(0, PACK_J, one_j, 0)


def contract_kernel(cap, r_ref, w_ref, o_ref, x_ref):
    found = pieces(cap)[0]
    for n, (_, fold, row, _) in enumerate(found):
        y = r_ref[:, row : row + 64 // fold, :]
        if fold > 1:
            group = lane_group(y.shape, LANES // fold)
            y = jnp.concatenate([jnp.where(group == g, y, jnp.zeros_like(y)) for g in range(fold)], axis=1)
        x_ref[:, LANES * n : LANES * (n + 1)] = y.reshape(ROWS * 64, LANES)
    p = jnp.dot(w_ref[...], x_ref[...], preferred_element_type=jnp.float32)
    for n, (_, fold, _, row) in enumerate(found):
        part = p[:, LANES * n : LANES * (n + 1)]
        if fold > 1:
            part = part + turn(part, 64)
        if fold > 2:
            part = part + turn(part, 32)
        height = 16 // fold
        part = part.reshape(ROWS, 16, LANES)
        out = part[:, :height]
        group = lane_group(out.shape, LANES // fold)
        for g in range(1, fold):
            out = jnp.where(group == g, part[:, height * g : height * (g + 1)], out)
        o_ref[:, row : row + height, :] = out.astype(jnp.bfloat16)


def prepare_kernel(mask_ref, jt_ref, oth_ref, row_ref, vr_ref, oths_ref, factor_ref):
    jt = jt_ref[0]
    low = lane_group((16, LANES), TILE) == 0

    def one_j(j, carry):
        oths_ref[j] = oth_ref[:, j].reshape(16, BV)
        row = row_ref[j]
        for lt in range(BV // LANES):
            sl = slice(LANES * lt, LANES * (lt + 1))
            k0 = mask_ref[jt, 2 * lt].astype(jnp.float32)
            k1 = mask_ref[jt, 2 * lt + 1].astype(jnp.float32)
            factor_ref[j, :, sl] = jnp.where(low, k0, k1) / (row - vr_ref[:, sl])
        return carry

    lax.fori_loop(0, NJ, one_j, 0)


def update_kernel(cap, repeated, mask_ref, jt_ref, c_ref, oths_ref, factor_ref, *refs):
    if repeated:
        before_ref, *refs = refs
    o_ref, comp_ref, res_ref, pos_ref = refs
    first = jt_ref[1]
    found = pieces(cap)[0]
    list_kept(mask_ref, jt_ref[0], None, pos_ref)
    low = lane_group((16, LANES), TILE) == 0

    def one_j(j, carry):
        for tile, fold, _, row in found:
            blocks = [c_ref[4 * j + q, row : row + 16 // fold, :].astype(jnp.float32) for q in range(4)]
            if fold == 1:
                for q in range(4):
                    comp_ref[tile // 2 + q] = blocks[q]
            elif fold == 2:
                m = lane_group((8, LANES), TILE) == 0
                for h in range(2):
                    f0, f1 = blocks[2 * h], blocks[2 * h + 1]
                    comp_ref[tile // 2 + h, 0:8, :] = jnp.where(m, f0, turn(f1, TILE))
                    comp_ref[tile // 2 + h, 8:16, :] = jnp.where(m, turn(f0, TILE), f1)
            else:
                group = lane_group((4, LANES), 32)
                for g in range(4):
                    out = turn(blocks[0], -32 * g)
                    for q in range(1, 4):
                        out = jnp.where(group == q, turn(blocks[q], 32 * (q - g)), out)
                    comp_ref[tile // 2, 4 * g : 4 * g + 4, :] = out
        for lt in range(BV // LANES):
            sl = slice(LANES * lt, LANES * (lt + 1))
            p0 = jnp.clip(pos_ref[2 * lt] - first, 0, cap - 1)
            p1 = jnp.clip(pos_ref[2 * lt + 1] - first, 0, cap - 1)
            a = pltpu.roll(comp_ref[p0 // 2], TILE * (p0 % 2), 1)
            b = pltpu.roll(comp_ref[p1 // 2], TILE * (1 - p1 % 2), 1)
            cycle = jnp.where(low, a, b)
            res_ref[:, sl] = factor_ref[j, :, sl] * (oths_ref[j, :, sl].astype(jnp.float32) + cycle)
        if repeated:
            done = before_ref[:, j].reshape(16, BV).astype(jnp.float32)
            for lt in range(BV // LANES):
                sl = slice(LANES * lt, LANES * (lt + 1))
                d0 = (pos_ref[2 * lt] < first).astype(jnp.int32)
                d1 = (pos_ref[2 * lt + 1] < first).astype(jnp.int32)
                res_ref[:, sl] = jnp.where(jnp.where(low, d0, d1) > 0, done[:, sl], res_ref[:, sl])
        o_ref[:, j] = res_ref[...].reshape(NI, 2, BV).astype(jnp.bfloat16)
        return carry

    lax.fori_loop(0, NJ, one_j, 0)


def one_pass(cap, before, amplitudes, integrals, others, levels, tile_mask, jt):
    found, rows_in, rows_out = pieces(cap)
    bf16 = jnp.bfloat16
    whole = pl.BlockSpec(memory_space=pltpu.VMEM)
    scalars = pl.BlockSpec(memory_space=pltpu.SMEM)
    packed = pl.pallas_call(
        functools.partial(pack_kernel, cap),
        out_shape=jax.ShapeDtypeStruct((ROWS, rows_in, LANES), bf16),
        grid_spec=pltpu.PrefetchScalarGridSpec(
            num_scalar_prefetch=2,
            grid=(NJ // PACK_J,),
            in_specs=[pl.BlockSpec((NK, PACK_J, 2, BV), lambda j, m, t: (0, j, 0, 0))],
            out_specs=pl.BlockSpec((4 * PACK_J, rows_in, LANES), lambda j, m, t: (j, 0, 0)),
            scratch_shapes=[pltpu.VMEM((2 * NK, BV), bf16), pltpu.SMEM((2 * NB,), jnp.int32)],
        ),
        name="pack",
    )(tile_mask, jt, amplitudes)
    received = lax.all_to_all(packed, "row", split_axis=0, concat_axis=0, tiled=True)

    own = integrals[:, :, 0, :].reshape(NI, ROWS, 2, TILE).transpose(3, 1, 0, 2).reshape(TILE, NI * TILE)
    gathered = lax.all_gather(own, "col", axis=0, tiled=False)
    by_row = gathered.reshape(NK, ROWS, 2, NI * TILE).transpose(1, 0, 2, 3).reshape(NK * TILE, NI * TILE)
    weights = by_row.T

    cycle = pl.pallas_call(
        functools.partial(contract_kernel, cap),
        out_shape=jax.ShapeDtypeStruct((ROWS, rows_out, LANES), bf16),
        in_specs=[whole, whole],
        out_specs=whole,
        scratch_shapes=[
            pltpu.VMEM((NK * TILE, LANES * len(found)), bf16),
        ],
        compiler_params=pltpu.CompilerParams(vmem_limit_bytes=40 << 20),
        name="contract",
    )(received, weights)
    returned = lax.all_to_all(cycle, "row", split_axis=0, concat_axis=0, tiled=True)

    occupied_left, occupied_right, virtual_left, virtual_right = levels
    row_term = (
        occupied_left[None, :, None] + occupied_right[:, None, None] - virtual_left[None, None, :]
    ).reshape(NJ, NI * 2)
    row_term = jnp.broadcast_to(row_term[:, :, None], (NJ, NI * 2, LANES))
    residual, factor = pl.pallas_call(
        prepare_kernel,
        out_shape=[
            jax.ShapeDtypeStruct((NJ, 2 * NI, BV), bf16),
            jax.ShapeDtypeStruct((NJ, 2 * NI, BV), jnp.float32),
        ],
        in_specs=[scalars, scalars, whole, whole, whole],
        out_specs=[whole, whole],
        compiler_params=pltpu.CompilerParams(vmem_limit_bytes=40 << 20),
        name="prepare",
    )(tile_mask, jt, others, row_term, virtual_right[None])

    return pl.pallas_call(
        functools.partial(update_kernel, cap, bool(before)),
        out_shape=jax.ShapeDtypeStruct(others.shape, bf16),
        in_specs=[scalars, scalars, whole, whole, whole] + [whole] * len(before),
        out_specs=whole,
        scratch_shapes=[
            pltpu.VMEM((cap // 2, 16, LANES), jnp.float32),
            pltpu.VMEM((16, BV), jnp.float32),
            pltpu.SMEM((NB,), jnp.int32),
        ],
        compiler_params=pltpu.CompilerParams(vmem_limit_bytes=40 << 20),
        name="update",
    )(tile_mask, jt, returned, residual, factor, *before)


def once(cap, most, jt, *arrays):
    return one_pass(cap, [], *arrays, jnp.stack([jt, jnp.int32(0)]))


def repeatedly(cap, most, jt, *arrays):
    def step(n, before):
        return one_pass(cap, [before], *arrays, jnp.stack([jt, n * cap]))

    passes = jnp.maximum((most + cap - 1) // cap, 1)
    return lax.fori_loop(0, passes, step, jnp.zeros_like(arrays[2]))


def shards(
    amplitudes,
    integrals,
    others,
    occupied_left,
    occupied_right,
    virtual_left,
    virtual_right,
    tile_mask,
):
    jt = (lax.axis_index("col") // (TILE // NJ)).astype(jnp.int32)
    chosen = pl.pallas_call(
        choose_kernel,
        out_shape=jax.ShapeDtypeStruct((2,), jnp.int32),
        in_specs=[pl.BlockSpec(memory_space=pltpu.SMEM)],
        out_specs=pl.BlockSpec(memory_space=pltpu.SMEM),
        name="choose",
    )(tile_mask)
    branch, most = chosen[0], chosen[1]
    steps = [functools.partial(once, cap) for cap in KEEP_CAPS[:-1]] + [functools.partial(repeatedly, KEEP_CAPS[-1])]
    return lax.switch(
        branch,
        steps,
        most,
        jt,
        amplitudes,
        integrals,
        others,
        (occupied_left, occupied_right, virtual_left, virtual_right),
        tile_mask,
    )


def solution(mesh):
    in_specs = (
        P(None, "col", "row", None),
        P(None, None, "col", None),
        P(None, "col", "row", None),
        P(),
        P("col"),
        P("row"),
        P(),
        P(),
    )
    out_specs = P(None, "col", "row", None)
    return jax.shard_map(shards, mesh=mesh, in_specs=in_specs, out_specs=out_specs, check_vma=False)
```

```python
import functools

import jax
import jax.numpy as jnp
from jax import lax
from jax.experimental import pallas as pl
from jax.experimental.pallas import tpu as pltpu
from jax.sharding import PartitionSpec as P

TILE = 64
LANES = 128
ROWS = 32
NI = 8
NJ = 8
NK = 32
PACK_J = 4
BV = 2048
NB = BV // TILE
KEEP_CAPS = (18, 20, 24)


def turn(v, by):
    by %= LANES
    return v if by == 0 else jnp.concatenate([v[..., LANES - by :], v[..., : LANES - by]], axis=-1)


def lane_group(shape, width):
    return lax.broadcasted_iota(jnp.int32, shape, len(shape) - 1) // width


def pieces(cap):
    found = []
    tile, row_in, row_out = 0, 0, 0
    for step, fold in [(8, 1)] * (cap // 8) + [(4, 2)] * (cap % 8 // 4) + [(2, 4)] * (cap % 4 // 2):
        found.append((tile, fold, row_in, row_out))
        tile, row_in, row_out = tile + step, row_in + 64 // fold, row_out + 16 // fold
    return found, row_in, row_out


def list_kept(mask_ref, jt, idx_ref, pos_ref):
    if idx_ref is not None:
        for t in range(2 * NB):
            idx_ref[t] = 0
    count = jnp.int32(0)
    for b in range(NB):
        if idx_ref is not None:
            idx_ref[count] = b
        if pos_ref is not None:
            pos_ref[b] = count
        count = count + jnp.minimum(mask_ref[jt, b], 1)


def choose_kernel(mask_ref, o_ref):
    most = jnp.int32(0)
    for row in range(mask_ref.shape[0]):
        most = jnp.maximum(most, sum(mask_ref[row, b] for b in range(NB)))
    o_ref[0] = sum((most > cap).astype(jnp.int32) for cap in KEEP_CAPS[:-1])
    o_ref[1] = most


def pack_kernel(cap, repeated, mask_ref, jt_ref, *refs):
    first = refs[0][0] if repeated else 0
    x_ref, o_ref, xs_ref, idx_ref = refs[repeated:]

    @pl.when(pl.program_id(0) == 0)
    def _():
        list_kept(mask_ref, jt_ref[0], idx_ref, None)

    def lanes_of(tile):
        return xs_ref[:, pl.ds(pl.multiple_of((tile // 2) * LANES, LANES), LANES)]

    def low(v, tile):
        return jnp.where(tile % 2 == 0, v, turn(v, TILE))

    def high(v, tile):
        return jnp.where(tile % 2 == 1, v, turn(v, TILE))

    def one_j(j, carry):
        xs_ref[...] = x_ref[:, j].reshape(2 * NK, BV)
        for tile, fold, row, _ in pieces(cap)[0]:
            for q in range(4):
                if fold == 1:
                    t0 = idx_ref[first + tile + 2 * q]
                    t1 = idx_ref[first + tile + 2 * q + 1]
                    parts = [low(lanes_of(t0), t0)[:, :TILE], high(lanes_of(t1), t1)[:, TILE:]]
                elif fold == 2:
                    t0 = idx_ref[first + tile + q]
                    v = lanes_of(t0)
                    parts = [low(v[:32], t0)[:, :TILE], high(v[32:], t0)[:, TILE:]]
                else:
                    t0 = idx_ref[first + tile + q // 2]
                    v = low(lanes_of(t0), t0)
                    parts = [turn(v[16 * g : 16 * g + 16], 32 * (g - q % 2))[:, 32 * g : 32 * g + 32] for g in range(4)]
                o_ref[4 * j + q, row : row + 64 // fold, :] = jnp.concatenate(parts, axis=1)
        return carry

    lax.fori_loop(0, PACK_J, one_j, 0)


def contract_kernel(cap, r_ref, w_ref, o_ref, x_ref):
    found = pieces(cap)[0]
    for n, (_, fold, row, _) in enumerate(found):
        y = r_ref[:, row : row + 64 // fold, :]
        if fold > 1:
            group = lane_group(y.shape, LANES // fold)
            y = jnp.concatenate([jnp.where(group == g, y, jnp.zeros_like(y)) for g in range(fold)], axis=1)
        x_ref[:, LANES * n : LANES * (n + 1)] = y.reshape(ROWS * 64, LANES)
    p = jnp.dot(w_ref[...], x_ref[...], preferred_element_type=jnp.float32)
    for n, (_, fold, _, row) in enumerate(found):
        part = p[:, LANES * n : LANES * (n + 1)]
        if fold > 1:
            part = part + turn(part, 64)
        if fold > 2:
            part = part + turn(part, 32)
        height = 16 // fold
        part = part.reshape(ROWS, 16, LANES)
        out = part[:, :height]
        group = lane_group(out.shape, LANES // fold)
        for g in range(1, fold):
            out = jnp.where(group == g, part[:, height * g : height * (g + 1)], out)
        o_ref[:, row : row + height, :] = out.astype(jnp.bfloat16)


def prepare_kernel(mask_ref, jt_ref, oth_ref, row_ref, vr_ref, oths_ref, factor_ref):
    jt = jt_ref[0]
    low = lane_group((16, LANES), TILE) == 0

    def one_j(j, carry):
        oths_ref[j] = oth_ref[:, j].reshape(16, BV)
        row = row_ref[j]
        for lt in range(BV // LANES):
            sl = slice(LANES * lt, LANES * (lt + 1))
            k0 = mask_ref[jt, 2 * lt].astype(jnp.float32)
            k1 = mask_ref[jt, 2 * lt + 1].astype(jnp.float32)
            factor_ref[j, :, sl] = jnp.where(low, k0, k1) / (row - vr_ref[:, sl])
        return carry

    lax.fori_loop(0, NJ, one_j, 0)


def update_kernel(cap, repeated, mask_ref, jt_ref, *refs):
    first = refs[0][0] if repeated else 0
    c_ref, oths_ref, factor_ref, *refs = refs[repeated:]
    if repeated:
        before_ref, *refs = refs
    o_ref, comp_ref, res_ref, pos_ref = refs
    found = pieces(cap)[0]
    list_kept(mask_ref, jt_ref[0], None, pos_ref)
    low = lane_group((16, LANES), TILE) == 0

    def one_j(j, carry):
        for tile, fold, _, row in found:
            blocks = [c_ref[4 * j + q, row : row + 16 // fold, :].astype(jnp.float32) for q in range(4)]
            if fold == 1:
                for q in range(4):
                    comp_ref[tile // 2 + q] = blocks[q]
            elif fold == 2:
                m = lane_group((8, LANES), TILE) == 0
                for h in range(2):
                    f0, f1 = blocks[2 * h], blocks[2 * h + 1]
                    comp_ref[tile // 2 + h, 0:8, :] = jnp.where(m, f0, turn(f1, TILE))
                    comp_ref[tile // 2 + h, 8:16, :] = jnp.where(m, turn(f0, TILE), f1)
            else:
                group = lane_group((4, LANES), 32)
                for g in range(4):
                    out = turn(blocks[0], -32 * g)
                    for q in range(1, 4):
                        out = jnp.where(group == q, turn(blocks[q], 32 * (q - g)), out)
                    comp_ref[tile // 2, 4 * g : 4 * g + 4, :] = out
        for lt in range(BV // LANES):
            sl = slice(LANES * lt, LANES * (lt + 1))
            p0 = jnp.clip(pos_ref[2 * lt] - first, 0, cap - 1)
            p1 = jnp.clip(pos_ref[2 * lt + 1] - first, 0, cap - 1)
            a = pltpu.roll(comp_ref[p0 // 2], TILE * (p0 % 2), 1)
            b = pltpu.roll(comp_ref[p1 // 2], TILE * (1 - p1 % 2), 1)
            cycle = jnp.where(low, a, b)
            res_ref[:, sl] = factor_ref[j, :, sl] * (oths_ref[j, :, sl].astype(jnp.float32) + cycle)
        if repeated:
            done = before_ref[:, j].reshape(16, BV).astype(jnp.float32)
            for lt in range(BV // LANES):
                sl = slice(LANES * lt, LANES * (lt + 1))
                d0 = (pos_ref[2 * lt] < first).astype(jnp.int32)
                d1 = (pos_ref[2 * lt + 1] < first).astype(jnp.int32)
                res_ref[:, sl] = jnp.where(jnp.where(low, d0, d1) > 0, done[:, sl], res_ref[:, sl])
        o_ref[:, j] = res_ref[...].reshape(NI, 2, BV).astype(jnp.bfloat16)
        return carry

    lax.fori_loop(0, NJ, one_j, 0, unroll=2)


def one_pass(cap, first, before, amplitudes, integrals, others, levels, tile_mask, jt):
    found, rows_in, rows_out = pieces(cap)
    bf16 = jnp.bfloat16
    repeated = len(first)
    whole = pl.BlockSpec(memory_space=pltpu.VMEM)
    scalars = pl.BlockSpec(memory_space=pltpu.SMEM)
    packed = pl.pallas_call(
        functools.partial(pack_kernel, cap, repeated),
        out_shape=jax.ShapeDtypeStruct((ROWS, rows_in, LANES), bf16),
        grid_spec=pltpu.PrefetchScalarGridSpec(
            num_scalar_prefetch=2 + repeated,
            grid=(NJ // PACK_J,),
            in_specs=[pl.BlockSpec((NK, PACK_J, 2, BV), lambda j, *_: (0, j, 0, 0))],
            out_specs=pl.BlockSpec((4 * PACK_J, rows_in, LANES), lambda j, *_: (j, 0, 0)),
            scratch_shapes=[pltpu.VMEM((2 * NK, BV), bf16), pltpu.SMEM((2 * NB,), jnp.int32)],
        ),
        name="pack",
    )(tile_mask, jt, *first, amplitudes)
    received = lax.all_to_all(packed, "row", split_axis=0, concat_axis=0, tiled=True)

    own = integrals[:, :, 0, :].reshape(NI, ROWS, 2, TILE).transpose(3, 1, 0, 2).reshape(TILE, NI * TILE)
    gathered = lax.all_gather(own, "col", axis=0, tiled=False)
    by_row = gathered.reshape(NK, ROWS, 2, NI * TILE).transpose(1, 0, 2, 3).reshape(NK * TILE, NI * TILE)
    weights = by_row.T

    cycle = pl.pallas_call(
        functools.partial(contract_kernel, cap),
        out_shape=jax.ShapeDtypeStruct((ROWS, rows_out, LANES), bf16),
        in_specs=[whole, whole],
        out_specs=whole,
        scratch_shapes=[
            pltpu.VMEM((NK * TILE, LANES * len(found)), bf16),
        ],
        compiler_params=pltpu.CompilerParams(vmem_limit_bytes=40 << 20),
        name="contract",
    )(received, weights)
    returned = lax.all_to_all(cycle, "row", split_axis=0, concat_axis=0, tiled=True)

    occupied_left, occupied_right, virtual_left, virtual_right = levels
    row_term = (
        occupied_left[None, :, None] + occupied_right[:, None, None] - virtual_left[None, None, :]
    ).reshape(NJ, NI * 2)
    row_term = jnp.broadcast_to(row_term[:, :, None], (NJ, NI * 2, LANES))
    residual, factor = pl.pallas_call(
        prepare_kernel,
        out_shape=[
            jax.ShapeDtypeStruct((NJ, 2 * NI, BV), bf16),
            jax.ShapeDtypeStruct((NJ, 2 * NI, BV), jnp.float32),
        ],
        in_specs=[scalars, scalars, whole, whole, whole],
        out_specs=[whole, whole],
        compiler_params=pltpu.CompilerParams(vmem_limit_bytes=40 << 20),
        name="prepare",
    )(tile_mask, jt, others, row_term, virtual_right[None])

    return pl.pallas_call(
        functools.partial(update_kernel, cap, repeated),
        out_shape=jax.ShapeDtypeStruct(others.shape, bf16),
        in_specs=[scalars] * (2 + repeated) + [whole] * (3 + len(before)),
        out_specs=whole,
        scratch_shapes=[
            pltpu.VMEM((cap // 2, 16, LANES), jnp.float32),
            pltpu.VMEM((16, BV), jnp.float32),
            pltpu.SMEM((NB,), jnp.int32),
        ],
        compiler_params=pltpu.CompilerParams(vmem_limit_bytes=40 << 20),
        name="update",
    )(tile_mask, jt, *first, returned, residual, factor, *before)


def once(cap, most, jt, *arrays):
    return one_pass(cap, [], [], *arrays, jt)


def repeatedly(cap, most, jt, *arrays):
    def step(n, before):
        return one_pass(cap, [(n * cap).reshape(1)], [before], *arrays, jt)

    passes = jnp.maximum((most + cap - 1) // cap, 1)
    return lax.fori_loop(0, passes, step, arrays[2])


def shards(
    amplitudes,
    integrals,
    others,
    occupied_left,
    occupied_right,
    virtual_left,
    virtual_right,
    tile_mask,
):
    jt = (lax.axis_index("col") // (TILE // NJ)).astype(jnp.int32).reshape(1)
    chosen = pl.pallas_call(
        choose_kernel,
        out_shape=jax.ShapeDtypeStruct((2,), jnp.int32),
        in_specs=[pl.BlockSpec(memory_space=pltpu.SMEM)],
        out_specs=pl.BlockSpec(memory_space=pltpu.SMEM),
        name="choose",
    )(tile_mask)
    branch, most = chosen[0], chosen[1]
    steps = [functools.partial(once, cap) for cap in KEEP_CAPS[:-1]] + [functools.partial(repeatedly, KEEP_CAPS[-1])]
    return lax.switch(
        branch,
        steps,
        most,
        jt,
        amplitudes,
        integrals,
        others,
        (occupied_left, occupied_right, virtual_left, virtual_right),
        tile_mask,
    )


def solution(mesh):
    in_specs = (
        P(None, "col", "row", None),
        P(None, None, "col", None),
        P(None, "col", "row", None),
        P(),
        P("col"),
        P("row"),
        P(),
        P(),
    )
    out_specs = P(None, "col", "row", None)
    return jax.shard_map(shards, mesh=mesh, in_specs=in_specs, out_specs=out_specs, check_vma=False)
```
